32 devices in a mesh: row: 16 (over z, x, core), col: 2 (over y).
Axes of the slice: x: 2, y: 2, z: 4, core: 2. Of those that a mesh axis runs over, the one named last changes fastest.
Arguments:
- g_occupied: bfloat16 [64, 512, 512], P(('row', 'col')), may hold values from -6 to 6
- g_virtual: bfloat16 [64, 512, 512], P(('row', 'col')), may hold values from -6 to 6
- owner: int32 [64, 1], P(('row', 'col')), may hold values from 0 to 1; in each aligned block of 2 rows (0 to 1, 2 to 3, ...) at most 2 rows name the same one
- coulomb: bfloat16 [1024, 3072], P('col', 'row'), may hold values from -0.25 to 0.25
Outputs:
- screened: bfloat16 [16384, 3072], P(('row', 'col'))
The draws below stay inside these ranges and needn't reach their ends.
Inputs may be any that keep to these rules, and one draw needn't show every extreme that they name: `owner`: among the 2 pairs of one device, no tile column is named more than twice, and some device names one twice.
All inputs are finite; a program needn't handle non-finite values.
Results may differ from the reference program's by a relative error of at most 0.015.
Values may be sent and summed in bfloat16 or wider, within the bound.
No kernel may reach another device: no remote copies, remote signals or barrier semaphores. Data moves between devices by JAX's collectives and lax.ppermute only.
A program may use at most 64 MiB of HBM per device.

```python
import math
import jax
import jax.numpy as jnp
import numpy as np
from jax import lax

B = 512
NS = 2
VC = 3072
PAIRS = 64
N_ROW = 16
N_COL = 2


def shard_levels(stream_key, shape, pieces, low, high):
    def one(dim, parts):
        draws = jax.random.uniform(jax.random.fold_in(jax.random.fold_in(stream_key, 6), dim), (parts,), jnp.float32, low / len(pieces), high / len(pieces))
        return jnp.repeat(jnp.exp(draws), shape[dim] // parts).reshape((-1,) + (1,) * (len(shape) - dim - 1))

    level = one(*pieces[0])
    for cut in pieces[1:]:
        level = level * one(*cut)
    return level


def assign_block(rng, own, number, rows, number_of, top, bound, lean):
    order = jax.random.permutation(rng, number_of)
    packed, ordinary = shares(number_of, rows * top, bound, lean, True), shares(number_of, rows * top, bound, lean, False)
    places = jnp.arange(number_of)

    def named(tallies, turn):
        used = int((tallies > 0).sum())
        fixed = max(1, used // 4)
        passed = fixed + (places - fixed + turn * (used - fixed)) % max(1, number_of - fixed)
        return jnp.zeros((number_of,), jnp.int32).at[order[jnp.where(places < fixed, places, passed)]].set(jnp.asarray(tallies, jnp.int32))

    tallies = jnp.where(number % 4 == 0, named(packed, number // 4), named(ordinary, number - number // 4 - 1))
    mixed = jax.random.permutation(jax.random.fold_in(own, 3), number_of)
    donor, taker = mixed[0:number_of // 2 * 2:2], mixed[1:number_of // 2 * 2:2]
    margin = jnp.minimum(tallies[donor] - 1, bound - tallies[taker]) // 2
    margin = jnp.where((donor == order[0]) | (taker == order[0]) | (tallies[taker] == 0), 0, jnp.maximum(margin, 0))
    passed = jax.random.randint(jax.random.fold_in(own, 4), (number_of // 2,), 0, 1 << 20) % (margin + 1)
    tallies = tallies.at[donor].add(-passed).at[taker].add(passed)
    members = jnp.searchsorted(jnp.cumsum(tallies), jnp.arange(rows * top), side="right").astype(jnp.int32)
    listing = members.reshape(top, rows).T
    listing = listing[jax.random.permutation(jax.random.fold_in(own, 1), rows)]
    turn = jax.random.randint(jax.random.fold_in(own, 2), (rows, 1), 0, top)
    return jnp.take_along_axis(listing, (jnp.arange(top)[None, :] + turn) % top, axis=1)


def shares(number_of, total, limit, lean, full):
    loads = [(1 << 20) // math.isqrt(rank ** lean) + 1 for rank in range(1, number_of + 1)]
    largest = limit if full else min(limit, max(-(-total // number_of), total * loads[0] // sum(loads)))
    least = 1 if total - largest >= number_of - 1 else 0
    given, spare = [largest] + [least] * (number_of - 1), total - largest - least * (number_of - 1)
    while spare > 0:
        candidates = [i for i in range(1, number_of) if given[i] < largest] or [i for i in range(1, number_of) if given[i] < limit]
        mass, budget = sum([loads[i] for i in candidates]), spare
        for i in candidates:
            more = min(limit - given[i], max(1, budget * loads[i] // mass), spare)
            given[i] = given[i] + more
            spare = spare - more
    return np.array(given)


def centred(key, extent, spread, reach, cuts=(), kind=jnp.bfloat16):
    entries = jax.random.normal(key, extent, jnp.float32) * spread
    if len(cuts) > 0:
        entries = shard_levels(key, extent, cuts, -0.22, 0.18) * entries
    return jnp.clip(entries, min=-reach, max=reach).astype(kind)


def setup_inputs(seed: int = 0) -> dict:
    splits = jax.random.split(jax.random.key(seed), 5)
    g_occupied = centred(splits[0], (PAIRS, B, B), 1.0, 6.0, ((0, 32),))
    g_virtual = centred(splits[1], (PAIRS, B, B), 1.0, 6.0, ((0, 32),))
    owner_keys = jax.random.split(jax.random.fold_in(splits[2], 1), PAIRS // NS)
    owner_turns = jax.random.permutation(jax.random.fold_in(splits[2], 3), PAIRS // NS)
    owner = jax.vmap(lambda own, number: assign_block(jax.random.fold_in(splits[2], 2), own, number, NS, N_COL, 1, 2, 2))(owner_keys, owner_turns).reshape((PAIRS, 1))
    coulomb = centred(splits[3], (N_COL * B, VC), B ** -0.5, 0.25, ((0, 2), (1, 16)))
    return {"g_occupied": g_occupied, "g_virtual": g_virtual, "owner": owner, "coulomb": coulomb}


def reference(g_occupied, g_virtual, owner, coulomb):
    n_row = N_ROW
    n_col = N_COL
    occ = g_occupied.reshape(n_row, n_col, NS, B, B)
    vir = g_virtual.reshape(n_row, n_col, NS, B, B)
    dest = owner.reshape(n_row, n_col, NS)
    panels = coulomb.reshape(n_col, B, VC).astype(jnp.float32)
    columns = jnp.arange(n_col, dtype=jnp.int32)

    def one_group(items):
        group_occ, group_vir, group_dest = items
        pol = group_occ.astype(jnp.float32) * group_vir.astype(jnp.float32)
        onehot = (group_dest[:, :, None] == columns[None, None, :]).astype(jnp.float32)
        contrib = jnp.einsum("csd,csij->cdij", onehot, pol).astype(jnp.bfloat16)
        tile = jnp.sum(contrib.astype(jnp.float32), axis=0).astype(jnp.bfloat16)
        result = jnp.einsum("dij,djk->dik", tile.astype(jnp.float32), panels)
        return result.astype(jnp.bfloat16)

    screened = lax.map(one_group, (occ, vir, dest))
    return screened.reshape(n_row * n_col * B, VC)
```

```python
import functools
import math

import jax
import jax.numpy as jnp
import numpy as np
from jax import lax
from jax.experimental import pallas as pl
from jax.experimental.pallas import tpu as pltpu
from jax.sharding import PartitionSpec as P

AXES = ("row", "col")


def chip_ring(mesh):
    n_row, n_col = mesh.devices.shape
    row_of = {}
    for r in range(n_row):
        for c in range(n_col):
            d = mesh.devices[r, c]
            row_of[(*d.coords, d.core_on_chip)] = (r, c)
    chips = sorted({k[:3] for k, (_, c) in row_of.items() if c == 0})
    if len(chips) * 2 != n_row:
        return None
    spans = [sorted({k[a] for k in chips}) for a in range(3)]
    wide = [a for a in range(3) if len(spans[a]) > 1]
    if len(wide) != 2 or math.prod(len(s) for s in spans) != len(chips):
        return None
    short, long = sorted(wide, key=lambda a: len(spans[a]))
    if len(spans[short]) != 2:
        return None
    lo, hi = spans[short]
    order = [(lo, v) for v in spans[long]] + [(hi, v) for v in reversed(spans[long])]
    place = {sv: i for i, sv in enumerate(order)}
    n = len(order)
    position = np.zeros((n_row, n_col), np.int32)
    core = np.zeros((n_row, n_col), np.int32)
    flat = {}
    for k, (r, c) in row_of.items():
        position[r, c] = place[(k[short], k[long])]
        core[r, c] = k[3]
        flat[(position[r, c], core[r, c], c)] = r * n_col + c
    slot = np.zeros((n_col, n), np.int32)
    for (p, k, c), f in flat.items():
        r = f // n_col
        if r % 2 != k:
            return None
        slot[c, p] = r // 2
    if (slot != slot[:1]).any():
        return None
    return n, position, core, flat, slot[0]


def matmul_kernel(n_chips, slots_ref, own_ref, recv_ref, *refs):
    pieces = refs[: 2 * n_chips]
    out_ref, panel, own, recv, tile, block, piece_sem, tile_sem, out_sem = refs[2 * n_chips :]
    width = 2 * panel.shape[2]
    cols = slots_ref.shape[0] // n_chips
    device = lax.axis_index("row")
    core = lax.rem(device, 2)
    base = device * n_chips

    def fetch(j, k):
        return pltpu.make_async_copy(pieces[2 * j + k], panel.at[j, k ^ core], piece_sem.at[j, k])

    def put(j):
        at = pl.multiple_of(slots_ref[base + j] * width, width)
        return pltpu.make_async_copy(block.at[j % 2], out_ref.at[:, pl.ds(at, width)], out_sem.at[j % 2])

    own_copy = pltpu.make_async_copy(own_ref, own, tile_sem.at[0])
    recv_copy = pltpu.make_async_copy(recv_ref, recv, tile_sem.at[1])
    own_copy.start()
    recv_copy.start()
    for j in range(n_chips):
        fetch(j, 0).start()
        fetch(j, 1).start()
    own_copy.wait()
    recv_copy.wait()
    tile[...] = (own[...].astype(jnp.float32) + recv[...].astype(jnp.float32)).astype(tile.dtype)
    for j in range(n_chips):
        fetch(j, 0).wait()
        fetch(j, 1).wait()
        if j >= 2:
            put(j - 2).wait()
        pair = panel[j].reshape(width, panel.shape[3])
        block[j % 2] = lax.dot_general(
            tile[...], pair, (((1,), (1,)), ((), ())), preferred_element_type=jnp.float32
        ).astype(block.dtype)
        put(j).start()
    put(n_chips - 2).wait()
    put(n_chips - 1).wait()


def ring_body(ring, g_occupied, g_virtual, owner, coulomb):
    n_chips, position, core, flat, slot = ring
    n_row, n_col = position.shape
    half = n_chips // 2

    def pairs(step):
        out = []
        for r in range(n_row):
            for c in range(n_col):
                p, k = step(int(position[r, c]), int(core[r, c]))
                out.append((r * n_col + c, flat[(p % n_chips, k, c)]))
        return out

    onward = pairs(lambda p, k: (p + 1 - 2 * k, k))
    across = pairs(lambda p, k: (p, 1 - k))

    me = lax.axis_index("col")
    pol = g_occupied.astype(jnp.float32) * g_virtual.astype(jnp.float32)

    def contribution(d):
        return jnp.sum(jnp.where(owner[:, :, None] == d, pol, 0.0), axis=0).astype(jnp.bfloat16)

    other = contribution(1 - me)
    own = contribution(me)
    received = lax.ppermute(other, "col", [(0, 1), (1, 0)])

    mine = coulomb.T
    sibling = lax.ppermute(mine, AXES, across)
    first, second = [mine], [sibling]
    for i in range(half):
        first.append(lax.ppermute(first[-1], AXES, onward))
        if i + 1 < half:
            second.append(lax.ppermute(second[-1], AXES, onward))
    pieces = [mine, sibling]
    for i in range(1, half + 1):
        a = lax.ppermute(first[i], AXES, across)
        if i < half:
            b = lax.ppermute(second[i], AXES, across)
            pieces += [first[i], second[i], b, a]
        else:
            pieces += [first[i], a]

    table = np.zeros((n_row, n_chips), np.int32)
    for r in range(n_row):
        p, way = int(position[r, 0]), 1 - 2 * int(core[r, 0])
        order = [p]
        for i in range(1, half + 1):
            order += [p - way * i, p + way * i] if i < half else [p - way * i]
        table[r] = [slot[q % n_chips] for q in order]

    width, depth = mine.shape
    rows = own.shape[0]
    any_spec = pl.BlockSpec(memory_space=pl.ANY)
    return pl.pallas_call(
        functools.partial(matmul_kernel, n_chips),
        out_shape=jax.ShapeDtypeStruct((rows, 2 * n_chips * width), jnp.bfloat16),
        in_specs=[pl.BlockSpec(memory_space=pltpu.SMEM)] + [any_spec] * (2 + 2 * n_chips),
        out_specs=any_spec,
        scratch_shapes=[
            pltpu.VMEM((n_chips, 2, width, depth), jnp.bfloat16),
            pltpu.VMEM((rows, depth), jnp.bfloat16),
            pltpu.VMEM((rows, depth), jnp.bfloat16),
            pltpu.VMEM((rows, depth), jnp.bfloat16),
            pltpu.VMEM((2, rows, 2 * width), jnp.bfloat16),
            pltpu.SemaphoreType.DMA((n_chips, 2)),
            pltpu.SemaphoreType.DMA((2,)),
            pltpu.SemaphoreType.DMA((2,)),
        ],
        compiler_params=pltpu.CompilerParams(vmem_limit_bytes=16 << 20),
        cost_estimate=pl.CostEstimate(
            flops=2 * rows * depth * 2 * n_chips * width,
            bytes_accessed=2 * n_chips * width * (rows + depth) * 2,
            transcendentals=0,
        ),
    )(jnp.asarray(table.reshape(-1)), own, received, *pieces)


def gather_body(g_occupied, g_virtual, owner, coulomb):
    n_col = lax.axis_size("col")
    pol = g_occupied.astype(jnp.float32) * g_virtual.astype(jnp.float32)
    columns = jnp.arange(n_col, dtype=jnp.int32)
    onehot = (owner[:, 0][:, None] == columns[None, :]).astype(jnp.float32)
    contrib = jnp.einsum("sd,sij->dij", onehot, pol).astype(jnp.bfloat16)
    received = lax.all_to_all(contrib, "col", split_axis=0, concat_axis=0, tiled=True)
    tile = jnp.sum(received.astype(jnp.float32), axis=0).astype(jnp.bfloat16)
    panel = lax.all_gather(coulomb, "row", axis=1, tiled=True)
    return jnp.dot(tile, panel, preferred_element_type=jnp.float32).astype(jnp.bfloat16)


def solution(mesh):
    ring = chip_ring(mesh) if mesh.shape["col"] == 2 else None
    return jax.shard_map(
        functools.partial(ring_body, ring) if ring else gather_body,
        mesh=mesh,
        in_specs=(P(AXES, None, None), P(AXES, None, None), P(AXES, None), P("col", "row")),
        out_specs=P(AXES, None),
        check_vma=False,
    )
```

```python
import functools
import math

import jax
import jax.numpy as jnp
import numpy as np
from jax import lax
from jax.experimental import pallas as pl
from jax.experimental.pallas import tpu as pltpu
from jax.sharding import PartitionSpec as P

AXES = ("row", "col")
ANY = pl.BlockSpec(memory_space=pl.ANY)
HBM = pl.BlockSpec(memory_space=pltpu.HBM)
VMEM = pl.BlockSpec(memory_space=pltpu.VMEM)

CHIPS = 8
ORDER = (
    "first_1",
    "first_2",
    "first_3",
    "first_4",
    "swap_0",
    "second_1",
    "second_2",
    "second_3",
    "tile",
    "swap_1_2_3",
    "chips_0_1_2",
    "swap_4",
    "chips_3_-1_-2_-3",
    "chips_4",
)
AFTER = {"swap_4": ("chips_0_1_2",), "second_1": ("own",)}
COST = {"chips_0_1_2": 64}


def chip_ring(mesh):
    n_row, n_col = mesh.devices.shape
    row_of = {}
    for r in range(n_row):
        for c in range(n_col):
            d = mesh.devices[r, c]
            row_of[(*d.coords, d.core_on_chip)] = (r, c)
    chips = sorted({k[:3] for k, (_, c) in row_of.items() if c == 0})
    if len(chips) * 2 != n_row:
        return None
    spans = [sorted({k[a] for k in chips}) for a in range(3)]
    wide = [a for a in range(3) if len(spans[a]) > 1]
    if len(wide) != 2 or math.prod(len(s) for s in spans) != len(chips):
        return None
    short, long = sorted(wide, key=lambda a: len(spans[a]))
    if len(spans[short]) != 2:
        return None
    lo, hi = spans[short]
    order = [(lo, v) for v in spans[long]] + [(hi, v) for v in reversed(spans[long])]
    place = {sv: i for i, sv in enumerate(order)}
    n = len(order)
    position = np.zeros((n_row, n_col), np.int32)
    core = np.zeros((n_row, n_col), np.int32)
    flat = {}
    for k, (r, c) in row_of.items():
        position[r, c] = place[(k[short], k[long])]
        core[r, c] = k[3]
        flat[(position[r, c], core[r, c], c)] = r * n_col + c
    slot = np.zeros((n_col, n), np.int32)
    for (p, k, c), f in flat.items():
        r = f // n_col
        if r % 2 != k:
            return None
        slot[c, p] = r // 2
    if (slot != slot[:1]).any():
        return None
    return n, position, core, flat, slot[0]


def contribution_kernel(parts, owner_ref, occ_ref, vir_ref, *refs):
    n_col = len(refs) - 3
    outs, (occ, vir, sem) = refs[:n_col], refs[n_col:]
    me = lax.axis_index("col")
    pairs, rows = occ.shape[0], occ.shape[1] // parts

    def fetch(i, ref, buf, k):
        at = pl.ds(i * rows, rows)
        return pltpu.make_async_copy(ref.at[:, at], buf.at[:, at], sem.at[i, k])

    for i in range(parts):
        fetch(i, occ_ref, occ, 0).start()
        fetch(i, vir_ref, vir, 1).start()
    for i in range(parts):
        fetch(i, occ_ref, occ, 0).wait()
        fetch(i, vir_ref, vir, 1).wait()
        at = pl.ds(i * rows, rows)
        pol = [occ[p, at].astype(jnp.float32) * vir[p, at].astype(jnp.float32) for p in range(pairs)]
        for k in range(n_col):
            column = lax.rem(me + k, n_col)
            total = jnp.where(owner_ref[0] == column, pol[0], 0.0)
            for p in range(1, pairs):
                total = total + jnp.where(owner_ref[p] == column, pol[p], 0.0)
            outs[k][at] = total.astype(outs[k].dtype)


def contributions(g_occupied, g_virtual, owner, n_col):
    pairs, rows, depth = g_occupied.shape
    parts = 4
    return pl.pallas_call(
        functools.partial(contribution_kernel, parts),
        out_shape=[jax.ShapeDtypeStruct((rows, depth), jnp.bfloat16)] * n_col,
        in_specs=[pl.BlockSpec(memory_space=pltpu.SMEM), HBM, HBM],
        out_specs=[VMEM] * n_col,
        scratch_shapes=[
            pltpu.VMEM(g_occupied.shape, g_occupied.dtype),
            pltpu.VMEM(g_virtual.shape, g_virtual.dtype),
            pltpu.SemaphoreType.DMA((parts, 2)),
        ],
        cost_estimate=pl.CostEstimate(
            flops=4 * pairs * rows * depth, bytes_accessed=4 * pairs * rows * depth, transcendentals=0
        ),
        name="contributions",
    )(owner.reshape(-1), g_occupied, g_virtual)


def columns_kernel(plan, parts, n_pieces, first, *refs):
    if first:
        own_ref, recv_ref, refs = refs[0], refs[1], refs[2:]
    else:
        tile_ref, refs = refs[0], refs[1:]
    pieces, refs = refs[:n_pieces], refs[n_pieces:]
    if first:
        out_ref, tile_ref, panel, block, sem = refs
    else:
        _, out_ref, panel, block, sem = refs
    shard = panel.shape[2]
    width = 2 * shard
    rows = block.shape[1] // parts
    device = lax.axis_index("row")
    core = lax.rem(device, 2)

    def put(j, i):
        slot = plan[j][0][0]
        for r, s in enumerate(plan[j][0]):
            slot = jnp.where(device == r, s, slot)
        at = pl.multiple_of(slot * width, width)
        span = pl.ds(i * rows, rows)
        return pltpu.make_async_copy(block.at[j, span], out_ref.at[span, pl.ds(at, width)], sem.at[j, i])

    if first:
        total = own_ref[...].astype(jnp.float32) + recv_ref[...].astype(jnp.float32)
        tile_ref[...] = total.astype(tile_ref.dtype)
    for j, (_, here, there) in enumerate(plan):
        panel[j, core] = pieces[here[0]][pl.ds(here[1], shard)]
        panel[j, 1 - core] = pieces[there[0]][pl.ds(there[1], shard)]
        pair = panel[j].reshape(width, panel.shape[3])
        for i in range(parts):
            span = pl.ds(i * rows, rows)
            block[j, span] = lax.dot_general(
                tile_ref[span], pair, (((1,), (1,)), ((), ())), preferred_element_type=jnp.float32
            ).astype(block.dtype)
            put(j, i).start()
    for j in range(len(plan)):
        for i in range(parts):
            put(j, i).wait()


def columns(plan, parts, tile_parts, pieces, shard, out, out_width, cost):
    first = out is None
    rows, depth = tile_parts[0].shape
    out_shape = [jax.ShapeDtypeStruct((rows, out_width), jnp.bfloat16)]
    out_specs = [ANY]
    if first:
        out_shape.append(jax.ShapeDtypeStruct((rows, depth), jnp.bfloat16))
        out_specs.append(VMEM)
    args = [*tile_parts, *pieces] + ([] if first else [out])
    width = 2 * shard
    result = pl.pallas_call(
        functools.partial(columns_kernel, plan, parts, len(pieces), first),
        out_shape=out_shape,
        in_specs=[VMEM] * (len(tile_parts) + len(pieces)) + [ANY] * (not first),
        out_specs=out_specs,
        scratch_shapes=[
            pltpu.VMEM((len(plan), 2, shard, depth), jnp.bfloat16),
            pltpu.VMEM((len(plan), rows, width), jnp.bfloat16),
            pltpu.SemaphoreType.DMA((len(plan), parts)),
        ],
        input_output_aliases={} if first else {len(args) - 1: 0},
        compiler_params=pltpu.CompilerParams(vmem_limit_bytes=24 << 20),
        cost_estimate=pl.CostEstimate(
            flops=cost * 2 * rows * depth * len(plan) * width,
            bytes_accessed=cost * len(plan) * width * rows * 2,
            transcendentals=0,
        ),
        name="columns",
    )(*args)
    return result if first else result[0]


def after(x, *done):
    return lax.optimization_barrier((x, *done))[0]


def ring_body(ring, g_occupied, g_virtual, owner, coulomb):
    n_chips, position, core, flat, slot = ring
    n_row, n_col = position.shape
    half = n_chips // 2

    def pairs(step):
        out = []
        for r in range(n_row):
            for c in range(n_col):
                p, k = step(int(position[r, c]), int(core[r, c]))
                out.append((r * n_col + c, flat[(p % n_chips, k, c)]))
        return out

    onward = pairs(lambda p, k: (p + 1 - 2 * k, k))
    across = pairs(lambda p, k: (p, 1 - k))
    over = [(r * n_col + c, r * n_col + 1 - c) for r in range(n_row) for c in range(n_col)]

    def places(step):
        out = []
        for r in range(n_row):
            p, way = int(position[r, 0]), 1 - 2 * int(core[r, 0])
            out.append(int(slot[(p - way * step) % n_chips]))
        return out

    own, other = contributions(g_occupied, g_virtual, owner, n_col)
    mine = coulomb.T
    shard = mine.shape[0]
    first, second, swapped = {0: mine}, {}, {}
    got = {"own": own}
    out, tile = None, None

    def moved(x, name, way):
        with jax.named_scope(name):
            got[name] = lax.ppermute(after(x, *(got[n] for n in AFTER.get(name, ()))), AXES, way)
        return got[name]

    for name in ORDER:
        kind, *rest = name.split("_")
        steps = [int(i) for i in rest]
        if kind == "first":
            first[steps[0]] = moved(first[steps[0] - 1], name, onward)
        elif kind == "second":
            second[steps[0]] = moved(second[steps[0] - 1], name, onward)
        elif kind == "tile":
            received = moved(other, name, over)
        elif kind == "swap":
            if steps == [0]:
                second[0] = moved(mine, name, across)
                continue
            parts = [x[i] for i in steps for x in ((first, second) if i < half else (first,))]
            both = moved(jnp.concatenate(parts), name, across)
            for n, i in enumerate(steps):
                swapped[i] = (both, 2 * n * shard)
        else:
            pieces, plan = [], []

            def add(x):
                if not any(x is y for y in pieces):
                    pieces.append(x)
                return next(n for n, y in enumerate(pieces) if x is y)

            for i in steps:
                if i == half:
                    plan.append((places(i), (add(first[i]), 0), (add(swapped[i][0]), swapped[i][1])))
                elif i >= 0:
                    plan.append((places(i), (add(first[i]), 0), (add(second[i]), 0)))
                else:
                    both, at = swapped[-i]
                    plan.append((places(i), (add(both), at + shard), (add(both), at)))
            parts = 4 if half in steps else 1
            terms = [own, received] if tile is None else [tile]
            result = columns(plan, parts, terms, pieces, shard, out, n_row * shard, COST.get(name, 1))
            if tile is None:
                result, tile = result
            out = result
            got[name] = tile if len(terms) == 2 else out
    return out


def gather_body(g_occupied, g_virtual, owner, coulomb):
    n_col = lax.axis_size("col")
    pol = g_occupied.astype(jnp.float32) * g_virtual.astype(jnp.float32)
    columns = jnp.arange(n_col, dtype=jnp.int32)
    onehot = (owner[:, 0][:, None] == columns[None, :]).astype(jnp.float32)
    contrib = jnp.einsum("sd,sij->dij", onehot, pol).astype(jnp.bfloat16)
    received = lax.all_to_all(contrib, "col", split_axis=0, concat_axis=0, tiled=True)
    tile = jnp.sum(received.astype(jnp.float32), axis=0).astype(jnp.bfloat16)
    panel = lax.all_gather(coulomb, "row", axis=1, tiled=True)
    return jnp.dot(tile, panel, preferred_element_type=jnp.float32).astype(jnp.bfloat16)


def solution(mesh):
    ring = chip_ring(mesh) if mesh.shape["col"] == 2 else None
    if ring and ring[0] != CHIPS:
        ring = None
    return jax.shard_map(
        functools.partial(ring_body, ring) if ring else gather_body,
        mesh=mesh,
        in_specs=(P(AXES, None, None), P(AXES, None, None), P(AXES, None), P("col", "row")),
        out_specs=P(AXES, None),
        check_vma=False,
    )
```

```python
import functools
import math

import jax
import jax.numpy as jnp
import numpy as np
from jax import lax
from jax.experimental import pallas as pl
from jax.experimental.pallas import tpu as pltpu
from jax.sharding import PartitionSpec as P

AXES = ("row", "col")
ANY = pl.BlockSpec(memory_space=pl.ANY)
HBM = pl.BlockSpec(memory_space=pltpu.HBM)
VMEM = pl.BlockSpec(memory_space=pltpu.VMEM)

CHIPS = 8
ORDER = (
    "first_1",
    "first_2",
    "first_3",
    "first_4",
    "swap_0",
    "second_1",
    "second_2",
    "second_3",
    "tile",
    "swap_1_2",
    "swap_3",
    "chips_0_1",
    "swap_4",
    "chips_2_3_-1_-2_-3",
    "chips_4",
)
AFTER = {"swap_4": ("chips_0_1",), "second_1": ("own",)}
COST = {"chips_0_1": 16}
FRONT = 3221225472


def chip_ring(mesh):
    n_row, n_col = mesh.devices.shape
    row_of = {}
    for r in range(n_row):
        for c in range(n_col):
            d = mesh.devices[r, c]
            row_of[(*d.coords, d.core_on_chip)] = (r, c)
    chips = sorted({k[:3] for k, (_, c) in row_of.items() if c == 0})
    if len(chips) * 2 != n_row:
        return None
    spans = [sorted({k[a] for k in chips}) for a in range(3)]
    wide = [a for a in range(3) if len(spans[a]) > 1]
    if len(wide) != 2 or math.prod(len(s) for s in spans) != len(chips):
        return None
    short, long = sorted(wide, key=lambda a: len(spans[a]))
    if len(spans[short]) != 2:
        return None
    lo, hi = spans[short]
    order = [(lo, v) for v in spans[long]] + [(hi, v) for v in reversed(spans[long])]
    place = {sv: i for i, sv in enumerate(order)}
    n = len(order)
    position = np.zeros((n_row, n_col), np.int32)
    core = np.zeros((n_row, n_col), np.int32)
    flat = {}
    for k, (r, c) in row_of.items():
        position[r, c] = place[(k[short], k[long])]
        core[r, c] = k[3]
        flat[(position[r, c], core[r, c], c)] = r * n_col + c
    slot = np.zeros((n_col, n), np.int32)
    for (p, k, c), f in flat.items():
        r = f // n_col
        if r % 2 != k:
            return None
        slot[c, p] = r // 2
    if (slot != slot[:1]).any():
        return None
    return n, position, core, flat, slot[0]


def tile_columns_kernel(n_col, out_ref):
    row = lax.broadcasted_iota(jnp.int32, out_ref.shape, 0)
    out_ref[...] = lax.rem(lax.axis_index("col") + row, n_col)


def tile_columns(n_col):
    return pl.pallas_call(
        functools.partial(tile_columns_kernel, n_col),
        out_shape=jax.ShapeDtypeStruct((8 * pl.cdiv(n_col, 8), 128), jnp.int32),
        out_specs=VMEM,
        cost_estimate=pl.CostEstimate(flops=FRONT, bytes_accessed=1 << 10, transcendentals=0),
        name="tile_columns",
    )()


def contribution_kernel(owner_ref, column_ref, occ_ref, vir_ref, *outs):
    pol = [occ_ref[p].astype(jnp.float32) * vir_ref[p].astype(jnp.float32) for p in range(occ_ref.shape[0])]
    lanes = column_ref.shape[1]
    for k, out in enumerate(outs):
        column = column_ref[pl.ds(k, 1)]
        picked = [jnp.where(owner_ref[:, p : p + 1] == column, 1.0, 0.0).astype(jnp.float32) for p in range(len(pol))]
        for at in range(0, out.shape[1], lanes):
            span = slice(at, at + lanes)
            total = pol[0][:, span] * picked[0]
            for p in range(1, len(pol)):
                total = total + pol[p][:, span] * picked[p]
            out[:, span] = total.astype(out.dtype)


def contributions(g_occupied, g_virtual, owner, column, n_col):
    pairs, rows, depth = g_occupied.shape
    return pl.pallas_call(
        contribution_kernel,
        out_shape=[jax.ShapeDtypeStruct((rows, depth), jnp.bfloat16)] * n_col,
        in_specs=[VMEM, VMEM, VMEM, VMEM],
        out_specs=[VMEM] * n_col,
        compiler_params=pltpu.CompilerParams(vmem_limit_bytes=24 << 20),
        cost_estimate=pl.CostEstimate(
            flops=4 * pairs * rows * depth, bytes_accessed=4 * pairs * rows * depth, transcendentals=0
        ),
        name="contributions",
    )(owner.reshape(1, pairs), column, g_occupied, g_virtual)


def columns_kernel(shape, n_terms, n_pieces, plan, held, last, *refs):
    device = lax.axis_index("row")
    core = lax.rem(device, 2)
    shard = shape[0]
    width = 2 * shard
    refs = list(refs)
    terms = [refs.pop(0) for _ in range(n_terms)]
    pieces = [refs.pop(0) for _ in range(n_pieces)]
    ready = refs.pop(0) if held else None
    sem, panel = refs.pop(), refs.pop()
    block = refs.pop()
    tile = terms[0] if n_terms == 1 else refs.pop()
    out = refs.pop() if refs else None

    def put(source, place, span, n):
        slot = place[0]
        for r, s in enumerate(place):
            slot = jnp.where(device == r, s, slot)
        at = pl.ds(pl.multiple_of(slot * width, width), width)
        return pltpu.make_async_copy(source.at[span], out.at[span, at], sem.at[n])

    copies = [put(ready.at[j], place, pl.ds(0, tile.shape[0]), j) for j, place in enumerate(held)]
    for c in copies:
        c.start()
    if n_terms == 2:
        tile[...] = (terms[0][...].astype(jnp.float32) + terms[1][...].astype(jnp.float32)).astype(tile.dtype)
    parts = 4 if last else 1
    rows = tile.shape[0] // parts
    for j, (place, here, there) in enumerate(plan):
        panel[j, core] = pieces[here[0]][pl.ds(here[1], shard)]
        panel[j, 1 - core] = pieces[there[0]][pl.ds(there[1], shard)]
        pair = panel[j].reshape(width, panel.shape[3])
        for i in range(parts):
            span = pl.ds(i * rows, rows)
            block[j, span] = lax.dot_general(
                tile[span], pair, (((1,), (1,)), ((), ())), preferred_element_type=jnp.float32
            ).astype(block.dtype)
            if last:
                copies.append(put(block.at[j], place, span, len(copies)))
                copies[-1].start()
    for c in copies:
        c.wait()


def columns(plan, terms, pieces, shard, ready, held, out, last, out_width, cost):
    rows, depth = terms[0].shape
    width = 2 * shard
    wide = jax.ShapeDtypeStruct((rows, out_width), jnp.bfloat16)
    blocks = (len(plan), rows, width)
    args = [*terms, *pieces]
    in_specs = [VMEM] * len(args)
    if held:
        args.append(ready)
        in_specs.append(VMEM)
    aliases = {}
    if out is not None:
        aliases = {len(args): 0}
        args.append(out)
        in_specs.append(ANY)
    out_shape, out_specs = [], []
    if held or last:
        out_shape.append(wide)
        out_specs.append(ANY)
    if len(terms) == 2:
        out_shape.append(jax.ShapeDtypeStruct((rows, depth), jnp.bfloat16))
        out_specs.append(VMEM)
    if not last:
        out_shape.append(jax.ShapeDtypeStruct(blocks, jnp.bfloat16))
        out_specs.append(VMEM)
    scratch = [pltpu.VMEM(blocks, jnp.bfloat16)] if last else []
    n_in = len(args)

    def body(*refs):
        refs = list(refs)
        if out is not None:
            del refs[n_in - 1]
        columns_kernel((shard, width), len(terms), len(pieces), plan, held, last, *refs)

    result = pl.pallas_call(
        body,
        out_shape=out_shape,
        in_specs=in_specs,
        out_specs=out_specs,
        scratch_shapes=scratch
        + [
            pltpu.VMEM((len(plan), 2, shard, depth), jnp.bfloat16),
            pltpu.SemaphoreType.DMA((len(held) + 4 * len(plan),)),
        ],
        input_output_aliases=aliases,
        compiler_params=pltpu.CompilerParams(vmem_limit_bytes=16 << 20),
        cost_estimate=pl.CostEstimate(
            flops=cost * 2 * rows * depth * len(plan) * width,
            bytes_accessed=cost * len(plan) * width * rows * 2,
            transcendentals=0,
        ),
        name="columns",
    )(*args)
    result = list(result)
    out = result.pop(0) if held or last else None
    tile = result.pop(0) if len(terms) == 2 else terms[0]
    return out, None if last else result.pop(0), tile


def after(x, *done):
    return lax.optimization_barrier((x, *done))[0]


def ring_body(ring, g_occupied, g_virtual, owner, coulomb):
    n_chips, position, core, flat, slot = ring
    n_row, n_col = position.shape
    half = n_chips // 2

    def pairs(step):
        out = []
        for r in range(n_row):
            for c in range(n_col):
                p, k = step(int(position[r, c]), int(core[r, c]))
                out.append((r * n_col + c, flat[(p % n_chips, k, c)]))
        return out

    onward = pairs(lambda p, k: (p + 1 - 2 * k, k))
    across = pairs(lambda p, k: (p, 1 - k))
    over = [(r * n_col + c, r * n_col + 1 - c) for r in range(n_row) for c in range(n_col)]

    def places(step):
        out = []
        for r in range(n_row):
            p, way = int(position[r, 0]), 1 - 2 * int(core[r, 0])
            out.append(int(slot[(p - way * step) % n_chips]))
        return out

    column = tile_columns(n_col)
    own, other = contributions(g_occupied, g_virtual, owner, column, n_col)
    mine = coulomb.T
    shard = mine.shape[0]
    first, second, swapped = {0: mine}, {}, {}
    got = {"own": own, "column": column}
    out, tile, ready, held = None, None, None, []

    def moved(x, name, way):
        with jax.named_scope(name):
            got[name] = lax.ppermute(after(x, *(got[n] for n in AFTER.get(name, ()))), AXES, way)
        return got[name]

    for name in ORDER:
        kind, *rest = name.split("_")
        steps = [int(i) for i in rest]
        if kind == "first":
            first[steps[0]] = moved(first[steps[0] - 1], name, onward)
        elif kind == "second":
            second[steps[0]] = moved(second[steps[0] - 1], name, onward)
        elif kind == "tile":
            received = moved(other, name, over)
        elif kind == "swap":
            if steps == [0]:
                second[0] = moved(mine, name, across)
                continue
            parts = [x[i] for i in steps for x in ((first, second) if i < half else (first,))]
            both = moved(jnp.concatenate(parts), name, across)
            for n, i in enumerate(steps):
                swapped[i] = (both, 2 * n * shard)
        else:
            pieces, plan = [], []

            def add(x):
                if not any(x is y for y in pieces):
                    pieces.append(x)
                return next(n for n, y in enumerate(pieces) if x is y)

            for i in steps:
                if i == half:
                    plan.append((places(i), (add(first[i]), 0), (add(swapped[i][0]), swapped[i][1])))
                elif i >= 0:
                    plan.append((places(i), (add(first[i]), 0), (add(second[i]), 0)))
                else:
                    both, at = swapped[-i]
                    plan.append((places(i), (add(both), at + shard), (add(both), at)))
            terms = [own, received] if tile is None else [tile]
            out, ready, tile = columns(
                plan, terms, pieces, shard, ready, held, out, half in steps, n_row * shard, COST.get(name, 1)
            )
            held = [place for place, _, _ in plan]
            got[name] = ready
    return out


def gather_body(g_occupied, g_virtual, owner, coulomb):
    n_col = lax.axis_size("col")
    pol = g_occupied.astype(jnp.float32) * g_virtual.astype(jnp.float32)
    columns = jnp.arange(n_col, dtype=jnp.int32)
    onehot = (owner[:, 0][:, None] == columns[None, :]).astype(jnp.float32)
    contrib = jnp.einsum("sd,sij->dij", onehot, pol).astype(jnp.bfloat16)
    received = lax.all_to_all(contrib, "col", split_axis=0, concat_axis=0, tiled=True)
    tile = jnp.sum(received.astype(jnp.float32), axis=0).astype(jnp.bfloat16)
    panel = lax.all_gather(coulomb, "row", axis=1, tiled=True)
    return jnp.dot(tile, panel, preferred_element_type=jnp.float32).astype(jnp.bfloat16)


def solution(mesh):
    ring = chip_ring(mesh) if mesh.shape["col"] == 2 else None
    if ring and ring[0] != CHIPS:
        ring = None
    return jax.shard_map(
        functools.partial(ring_body, ring) if ring else gather_body,
        mesh=mesh,
        in_specs=(P(AXES, None, None), P(AXES, None, None), P(AXES, None), P("col", "row")),
        out_specs=P(AXES, None),
        check_vma=False,
    )
```

```python
import functools
import math

import jax
import jax.numpy as jnp
import numpy as np
from jax import lax
from jax.experimental import pallas as pl
from jax.experimental.pallas import tpu as pltpu
from jax.sharding import PartitionSpec as P

AXES = ("row", "col")
ANY = pl.BlockSpec(memory_space=pl.ANY)
HBM = pl.BlockSpec(memory_space=pltpu.HBM)
VMEM = pl.BlockSpec(memory_space=pltpu.VMEM)

CHIPS = 8
ORDER = (
    "first_1",
    "first_2",
    "first_3",
    "first_4",
    "swap_0",
    "second_1",
    "second_2",
    "second_3",
    "tile",
    "swap_1_2",
    "swap_3",
    "chips_0_1_2_3",
    "swap_4",
    "chips_-1_-2_-3",
    "chips_4",
)
AFTER = {"swap_4": ("chips_0_1_2_3",), "second_1": ("own",)}
COST = {"chips_0_1_2_3": 8}
FRONT = 3221225472
DIRECT = 2


def chip_ring(mesh):
    n_row, n_col = mesh.devices.shape
    row_of = {}
    for r in range(n_row):
        for c in range(n_col):
            d = mesh.devices[r, c]
            row_of[(*d.coords, d.core_on_chip)] = (r, c)
    chips = sorted({k[:3] for k, (_, c) in row_of.items() if c == 0})
    if len(chips) * 2 != n_row:
        return None
    spans = [sorted({k[a] for k in chips}) for a in range(3)]
    wide = [a for a in range(3) if len(spans[a]) > 1]
    if len(wide) != 2 or math.prod(len(s) for s in spans) != len(chips):
        return None
    short, long = sorted(wide, key=lambda a: len(spans[a]))
    if len(spans[short]) != 2:
        return None
    lo, hi = spans[short]
    order = [(lo, v) for v in spans[long]] + [(hi, v) for v in reversed(spans[long])]
    place = {sv: i for i, sv in enumerate(order)}
    n = len(order)
    position = np.zeros((n_row, n_col), np.int32)
    core = np.zeros((n_row, n_col), np.int32)
    flat = {}
    for k, (r, c) in row_of.items():
        position[r, c] = place[(k[short], k[long])]
        core[r, c] = k[3]
        flat[(position[r, c], core[r, c], c)] = r * n_col + c
    slot = np.zeros((n_col, n), np.int32)
    for (p, k, c), f in flat.items():
        r = f // n_col
        if r % 2 != k:
            return None
        slot[c, p] = r // 2
    if (slot != slot[:1]).any():
        return None
    return n, position, core, flat, slot[0]


def tile_columns_kernel(n_col, out_ref):
    row = lax.broadcasted_iota(jnp.int32, out_ref.shape, 0)
    out_ref[...] = lax.rem(lax.axis_index("col") + row, n_col)


def tile_columns(n_col):
    return pl.pallas_call(
        functools.partial(tile_columns_kernel, n_col),
        out_shape=jax.ShapeDtypeStruct((8 * pl.cdiv(n_col, 8), 128), jnp.int32),
        out_specs=VMEM,
        cost_estimate=pl.CostEstimate(flops=FRONT, bytes_accessed=1 << 10, transcendentals=0),
        name="tile_columns",
    )()


def contribution_kernel(owner_ref, column_ref, occ_ref, vir_ref, *outs):
    pol = [occ_ref[p].astype(jnp.float32) * vir_ref[p].astype(jnp.float32) for p in range(occ_ref.shape[0])]
    lanes = column_ref.shape[1]
    for k, out in enumerate(outs):
        column = column_ref[pl.ds(k, 1)]
        picked = [jnp.where(owner_ref[:, p : p + 1] == column, 1.0, 0.0).astype(jnp.float32) for p in range(len(pol))]
        for at in range(0, out.shape[1], lanes):
            span = slice(at, at + lanes)
            total = pol[0][:, span] * picked[0]
            for p in range(1, len(pol)):
                total = total + pol[p][:, span] * picked[p]
            out[:, span] = total.astype(out.dtype)


def contributions(g_occupied, g_virtual, owner, column, n_col):
    pairs, rows, depth = g_occupied.shape
    return pl.pallas_call(
        contribution_kernel,
        out_shape=[jax.ShapeDtypeStruct((rows, depth), jnp.bfloat16)] * n_col,
        in_specs=[VMEM, VMEM, VMEM, VMEM],
        out_specs=[VMEM] * n_col,
        compiler_params=pltpu.CompilerParams(vmem_limit_bytes=24 << 20),
        cost_estimate=pl.CostEstimate(
            flops=4 * pairs * rows * depth, bytes_accessed=4 * pairs * rows * depth, transcendentals=0
        ),
        name="contributions",
    )(owner.reshape(1, pairs), column, g_occupied, g_virtual)


def columns_kernel(shard, n_terms, n_pieces, plan, direct, held, last, *refs):
    device = lax.axis_index("row")
    core = lax.rem(device, 2)
    width = 2 * shard
    refs = list(refs)
    terms = [refs.pop(0) for _ in range(n_terms)]
    pieces = [refs.pop(0) for _ in range(n_pieces)]
    ready = [refs.pop(0) for _ in held]
    sem, panel = refs.pop(), refs.pop()
    block = refs.pop()
    tile = terms[0] if n_terms == 1 else refs.pop()
    out = refs.pop() if refs else None
    copies = []

    def put(source, place, span):
        slot = place[0]
        for r, s in enumerate(place):
            slot = jnp.where(device == r, s, slot)
        at = pl.ds(pl.multiple_of(slot * width, width), width)
        copies.append(pltpu.make_async_copy(source.at[span], out.at[span, at], sem.at[len(copies)]))
        copies[-1].start()

    for blocks, places in zip(ready, held, strict=True):
        for j, place in places:
            put(blocks.at[j], place, pl.ds(0, tile.shape[0]))
    if n_terms == 2:
        tile[...] = (terms[0][...].astype(jnp.float32) + terms[1][...].astype(jnp.float32)).astype(tile.dtype)
    parts = 4 if last else 1
    rows = tile.shape[0] // parts
    for j, (place, here, there) in enumerate(plan):
        panel[j, core] = pieces[here[0]][pl.ds(here[1], shard)]
        panel[j, 1 - core] = pieces[there[0]][pl.ds(there[1], shard)]
        pair = panel[j].reshape(width, panel.shape[3])
        for i in range(parts):
            span = pl.ds(i * rows, rows)
            block[j, span] = lax.dot_general(
                tile[span], pair, (((1,), (1,)), ((), ())), preferred_element_type=jnp.float32
            ).astype(block.dtype)
            if j < direct:
                put(block.at[j], place, span)
    for c in copies:
        c.wait()


def columns(plan, terms, pieces, shard, direct, ready, held, out, last, out_width, cost):
    rows, depth = terms[0].shape
    width = 2 * shard
    blocks = (len(plan), rows, width)
    args = [*terms, *pieces, *ready]
    in_specs = [VMEM] * len(args)
    aliases = {}
    if last and out is not None:
        aliases = {len(args): 0}
        args.append(out)
        in_specs.append(ANY)
    out_shape, out_specs = [], []
    if direct:
        out_shape.append(jax.ShapeDtypeStruct((rows, out_width), jnp.bfloat16))
        out_specs.append(ANY)
    if len(terms) == 2:
        out_shape.append(jax.ShapeDtypeStruct((rows, depth), jnp.bfloat16))
        out_specs.append(VMEM)
    if not last:
        out_shape.append(jax.ShapeDtypeStruct(blocks, jnp.bfloat16))
        out_specs.append(VMEM)
    n_in = len(args)

    def body(*refs):
        refs = list(refs)
        if aliases:
            del refs[n_in - 1]
        columns_kernel(shard, len(terms), len(pieces), plan, direct, held, last, *refs)

    result = pl.pallas_call(
        body,
        out_shape=out_shape,
        in_specs=in_specs,
        out_specs=out_specs,
        scratch_shapes=([pltpu.VMEM(blocks, jnp.bfloat16)] if last else [])
        + [
            pltpu.VMEM((len(plan), 2, shard, depth), jnp.bfloat16),
            pltpu.SemaphoreType.DMA((sum(len(h) for h in held) + 4 * len(plan),)),
        ],
        input_output_aliases=aliases,
        compiler_params=pltpu.CompilerParams(vmem_limit_bytes=16 << 20),
        cost_estimate=pl.CostEstimate(
            flops=cost * 2 * rows * depth * len(plan) * width,
            bytes_accessed=cost * len(plan) * width * rows * 2,
            transcendentals=0,
        ),
        name="columns",
    )(*args)
    result = list(result)
    out = result.pop(0) if direct else out
    tile = result.pop(0) if len(terms) == 2 else terms[0]
    return out, None if last else result.pop(0), tile


def after(x, *done):
    return lax.optimization_barrier((x, *done))[0]


def ring_body(ring, g_occupied, g_virtual, owner, coulomb):
    n_chips, position, core, flat, slot = ring
    n_row, n_col = position.shape
    half = n_chips // 2

    def pairs(step):
        out = []
        for r in range(n_row):
            for c in range(n_col):
                p, k = step(int(position[r, c]), int(core[r, c]))
                out.append((r * n_col + c, flat[(p % n_chips, k, c)]))
        return out

    onward = pairs(lambda p, k: (p + 1 - 2 * k, k))
    across = pairs(lambda p, k: (p, 1 - k))
    over = [(r * n_col + c, r * n_col + 1 - c) for r in range(n_row) for c in range(n_col)]

    def places(step):
        out = []
        for r in range(n_row):
            p, way = int(position[r, 0]), 1 - 2 * int(core[r, 0])
            out.append(int(slot[(p - way * step) % n_chips]))
        return out

    column = tile_columns(n_col)
    own, other = contributions(g_occupied, g_virtual, owner, column, n_col)
    mine = coulomb.T
    shard = mine.shape[0]
    first, second, swapped = {0: mine}, {}, {}
    got = {"own": own, "column": column}
    out, tile, ready, held = None, None, [], []

    def moved(x, name, way):
        with jax.named_scope(name):
            got[name] = lax.ppermute(after(x, *(got[n] for n in AFTER.get(name, ()))), AXES, way)
        return got[name]

    for name in ORDER:
        kind, *rest = name.split("_")
        steps = [int(i) for i in rest]
        if kind == "first":
            first[steps[0]] = moved(first[steps[0] - 1], name, onward)
        elif kind == "second":
            second[steps[0]] = moved(second[steps[0] - 1], name, onward)
        elif kind == "tile":
            received = moved(other, name, over)
        elif kind == "swap":
            if steps == [0]:
                second[0] = moved(mine, name, across)
                continue
            parts = [x[i] for i in steps for x in ((first, second) if i < half else (first,))]
            both = moved(jnp.concatenate(parts), name, across)
            for n, i in enumerate(steps):
                swapped[i] = (both, 2 * n * shard)
        else:
            pieces, plan = [], []

            def add(x):
                if not any(x is y for y in pieces):
                    pieces.append(x)
                return next(n for n, y in enumerate(pieces) if x is y)

            for i in steps:
                if i == half:
                    plan.append((places(i), (add(first[i]), 0), (add(swapped[i][0]), swapped[i][1])))
                elif i >= 0:
                    plan.append((places(i), (add(first[i]), 0), (add(second[i]), 0)))
                else:
                    both, at = swapped[-i]
                    plan.append((places(i), (add(both), at + shard), (add(both), at)))
            terms = [own, received] if tile is None else [tile]
            last = half in steps
            direct = len(plan) if last else DIRECT if tile is None else 0
            out, blocks, tile = columns(
                plan, terms, pieces, shard, direct, ready if last else [], held if last else [], out, last,
                n_row * shard, COST.get(name, 1),
            )
            ready.append(blocks)
            held.append([(j, plan[j][0]) for j in range(direct, len(plan))])
            got[name] = blocks
    return out


def gather_body(g_occupied, g_virtual, owner, coulomb):
    n_col = lax.axis_size("col")
    pol = g_occupied.astype(jnp.float32) * g_virtual.astype(jnp.float32)
    columns = jnp.arange(n_col, dtype=jnp.int32)
    onehot = (owner[:, 0][:, None] == columns[None, :]).astype(jnp.float32)
    contrib = jnp.einsum("sd,sij->dij", onehot, pol).astype(jnp.bfloat16)
    received = lax.all_to_all(contrib, "col", split_axis=0, concat_axis=0, tiled=True)
    tile = jnp.sum(received.astype(jnp.float32), axis=0).astype(jnp.bfloat16)
    panel = lax.all_gather(coulomb, "row", axis=1, tiled=True)
    return jnp.dot(tile, panel, preferred_element_type=jnp.float32).astype(jnp.bfloat16)


def solution(mesh):
    ring = chip_ring(mesh) if mesh.shape["col"] == 2 else None
    if ring and ring[0] != CHIPS:
        ring = None
    return jax.shard_map(
        functools.partial(ring_body, ring) if ring else gather_body,
        mesh=mesh,
        in_specs=(P(AXES, None, None), P(AXES, None, None), P(AXES, None), P("col", "row")),
        out_specs=P(AXES, None),
        check_vma=False,
    )
```

```python
import functools
import math

import jax
import jax.numpy as jnp
import numpy as np
from jax import lax
from jax.experimental import pallas as pl
from jax.experimental.pallas import tpu as pltpu
from jax.sharding import PartitionSpec as P

AXES = ("row", "col")
ANY = pl.BlockSpec(memory_space=pl.ANY)
HBM = pl.BlockSpec(memory_space=pltpu.HBM)
VMEM = pl.BlockSpec(memory_space=pltpu.VMEM)

CHIPS = 8
ORDER = (
    "first_1",
    "first_2",
    "first_3",
    "first_4",
    "swap_0",
    "second_1",
    "second_2",
    "second_3",
    "tile",
    "swap_1_2",
    "swap_3",
    "chips_0_1_2_3",
    "swap_4",
    "chips_-1_-2_-3",
    "chips_4",
)
AFTER = {"swap_4": ("chips_0_1_2_3",), "first_2": ("own",)}
COST = {"chips_0_1_2_3": 8}
FRONT = 3221225472
DIRECT = 2


def chip_ring(mesh):
    n_row, n_col = mesh.devices.shape
    row_of = {}
    for r in range(n_row):
        for c in range(n_col):
            d = mesh.devices[r, c]
            row_of[(*d.coords, d.core_on_chip)] = (r, c)
    chips = sorted({k[:3] for k, (_, c) in row_of.items() if c == 0})
    if len(chips) * 2 != n_row:
        return None
    spans = [sorted({k[a] for k in chips}) for a in range(3)]
    wide = [a for a in range(3) if len(spans[a]) > 1]
    if len(wide) != 2 or math.prod(len(s) for s in spans) != len(chips):
        return None
    short, long = sorted(wide, key=lambda a: len(spans[a]))
    if len(spans[short]) != 2:
        return None
    lo, hi = spans[short]
    order = [(lo, v) for v in spans[long]] + [(hi, v) for v in reversed(spans[long])]
    place = {sv: i for i, sv in enumerate(order)}
    n = len(order)
    position = np.zeros((n_row, n_col), np.int32)
    core = np.zeros((n_row, n_col), np.int32)
    flat = {}
    for k, (r, c) in row_of.items():
        position[r, c] = place[(k[short], k[long])]
        core[r, c] = k[3]
        flat[(position[r, c], core[r, c], c)] = r * n_col + c
    slot = np.zeros((n_col, n), np.int32)
    for (p, k, c), f in flat.items():
        r = f // n_col
        if r % 2 != k:
            return None
        slot[c, p] = r // 2
    if (slot != slot[:1]).any():
        return None
    return n, position, core, flat, slot[0]


def tile_columns_kernel(n_col, out_ref):
    row = lax.broadcasted_iota(jnp.int32, out_ref.shape, 0)
    out_ref[...] = lax.rem(lax.axis_index("col") + row, n_col)


def tile_columns(n_col):
    return pl.pallas_call(
        functools.partial(tile_columns_kernel, n_col),
        out_shape=jax.ShapeDtypeStruct((8 * pl.cdiv(n_col, 8), 128), jnp.int32),
        out_specs=VMEM,
        cost_estimate=pl.CostEstimate(flops=FRONT, bytes_accessed=1 << 10, transcendentals=0),
        name="tile_columns",
    )()


def contribution_kernel(owner_ref, column_ref, occ_ref, vir_ref, *outs):
    pol = [occ_ref[p].astype(jnp.float32) * vir_ref[p].astype(jnp.float32) for p in range(occ_ref.shape[0])]
    lanes = column_ref.shape[1]
    for k, out in enumerate(outs):
        column = column_ref[pl.ds(k, 1)]
        picked = [jnp.where(owner_ref[:, p : p + 1] == column, 1.0, 0.0).astype(jnp.float32) for p in range(len(pol))]
        for at in range(0, out.shape[1], lanes):
            span = slice(at, at + lanes)
            total = pol[0][:, span] * picked[0]
            for p in range(1, len(pol)):
                total = total + pol[p][:, span] * picked[p]
            out[:, span] = total.astype(out.dtype)


def contributions(g_occupied, g_virtual, owner, column, n_col):
    pairs, rows, depth = g_occupied.shape
    return pl.pallas_call(
        contribution_kernel,
        out_shape=[jax.ShapeDtypeStruct((rows, depth), jnp.bfloat16)] * n_col,
        in_specs=[VMEM, VMEM, VMEM, VMEM],
        out_specs=[VMEM] * n_col,
        compiler_params=pltpu.CompilerParams(vmem_limit_bytes=24 << 20),
        cost_estimate=pl.CostEstimate(
            flops=4 * pairs * rows * depth, bytes_accessed=4 * pairs * rows * depth, transcendentals=0
        ),
        name="contributions",
    )(owner.reshape(1, pairs), column, g_occupied, g_virtual)


def columns_kernel(shard, n_terms, n_pieces, plan, direct, held, last, *refs):
    device = lax.axis_index("row")
    core = lax.rem(device, 2)
    width = 2 * shard
    refs = list(refs)
    terms = [refs.pop(0) for _ in range(n_terms)]
    pieces = [refs.pop(0) for _ in range(n_pieces)]
    ready = [refs.pop(0) for _ in held]
    sem, panel = refs.pop(), refs.pop()
    block = refs.pop()
    tile = terms[0] if n_terms == 1 else refs.pop()
    out = refs.pop() if refs else None
    copies = []

    def put(source, place, span):
        slot = place[0]
        for r, s in enumerate(place):
            slot = jnp.where(device == r, s, slot)
        at = pl.ds(pl.multiple_of(slot * width, width), width)
        copies.append(pltpu.make_async_copy(source.at[span], out.at[span, at], sem.at[len(copies)]))
        copies[-1].start()

    for blocks, places in zip(ready, held, strict=True):
        for j, place in places:
            put(blocks.at[j], place, pl.ds(0, tile.shape[0]))
    if n_terms == 2:
        tile[...] = (terms[0][...].astype(jnp.float32) + terms[1][...].astype(jnp.float32)).astype(tile.dtype)
    parts = 4 if last else 1
    rows = tile.shape[0] // parts
    for j, (place, here, there) in enumerate(plan):
        panel[j, core] = pieces[here[0]][pl.ds(here[1], shard)]
        panel[j, 1 - core] = pieces[there[0]][pl.ds(there[1], shard)]
        pair = panel[j].reshape(width, panel.shape[3])
        for i in range(parts):
            span = pl.ds(i * rows, rows)
            block[j, span] = lax.dot_general(
                tile[span], pair, (((1,), (1,)), ((), ())), preferred_element_type=jnp.float32
            ).astype(block.dtype)
            if j < direct:
                put(block.at[j], place, span)
    for c in copies:
        c.wait()


def columns(plan, terms, pieces, shard, direct, ready, held, out, last, out_width, cost):
    rows, depth = terms[0].shape
    width = 2 * shard
    blocks = (len(plan), rows, width)
    args = [*terms, *pieces, *ready]
    in_specs = [VMEM] * len(args)
    aliases = {}
    if last and out is not None:
        aliases = {len(args): 0}
        args.append(out)
        in_specs.append(ANY)
    out_shape, out_specs = [], []
    if direct:
        out_shape.append(jax.ShapeDtypeStruct((rows, out_width), jnp.bfloat16))
        out_specs.append(ANY)
    if len(terms) == 2:
        out_shape.append(jax.ShapeDtypeStruct((rows, depth), jnp.bfloat16))
        out_specs.append(VMEM)
    if not last:
        out_shape.append(jax.ShapeDtypeStruct(blocks, jnp.bfloat16))
        out_specs.append(VMEM)
    n_in = len(args)

    def body(*refs):
        refs = list(refs)
        if aliases:
            del refs[n_in - 1]
        columns_kernel(shard, len(terms), len(pieces), plan, direct, held, last, *refs)

    result = pl.pallas_call(
        body,
        out_shape=out_shape,
        in_specs=in_specs,
        out_specs=out_specs,
        scratch_shapes=([pltpu.VMEM(blocks, jnp.bfloat16)] if last else [])
        + [
            pltpu.VMEM((len(plan), 2, shard, depth), jnp.bfloat16),
            pltpu.SemaphoreType.DMA((sum(len(h) for h in held) + 4 * len(plan),)),
        ],
        input_output_aliases=aliases,
        compiler_params=pltpu.CompilerParams(vmem_limit_bytes=16 << 20),
        cost_estimate=pl.CostEstimate(
            flops=cost * 2 * rows * depth * len(plan) * width,
            bytes_accessed=cost * len(plan) * width * rows * 2,
            transcendentals=0,
        ),
        name="columns",
    )(*args)
    result = list(result)
    out = result.pop(0) if direct else out
    tile = result.pop(0) if len(terms) == 2 else terms[0]
    return out, None if last else result.pop(0), tile


def after(x, *done):
    return lax.optimization_barrier((x, *done))[0]


def ring_body(ring, g_occupied, g_virtual, owner, coulomb):
    n_chips, position, core, flat, slot = ring
    n_row, n_col = position.shape
    half = n_chips // 2

    def pairs(step):
        out = []
        for r in range(n_row):
            for c in range(n_col):
                p, k = step(int(position[r, c]), int(core[r, c]))
                out.append((r * n_col + c, flat[(p % n_chips, k, c)]))
        return out

    onward = pairs(lambda p, k: (p + 1 - 2 * k, k))
    across = pairs(lambda p, k: (p, 1 - k))
    over = [(r * n_col + c, r * n_col + 1 - c) for r in range(n_row) for c in range(n_col)]

    def places(step):
        out = []
        for r in range(n_row):
            p, way = int(position[r, 0]), 1 - 2 * int(core[r, 0])
            out.append(int(slot[(p - way * step) % n_chips]))
        return out

    column = tile_columns(n_col)
    own, other = contributions(g_occupied, g_virtual, owner, column, n_col)
    mine = coulomb.T
    shard = mine.shape[0]
    first, second, swapped = {0: mine}, {}, {}
    got = {"own": own, "column": column}
    out, tile, ready, held = None, None, [], []

    def moved(x, name, way):
        with jax.named_scope(name):
            got[name] = lax.ppermute(after(x, *(got[n] for n in AFTER.get(name, ()))), AXES, way)
        return got[name]

    for name in ORDER:
        kind, *rest = name.split("_")
        steps = [int(i) for i in rest]
        if kind == "first":
            first[steps[0]] = moved(first[steps[0] - 1], name, onward)
        elif kind == "second":
            second[steps[0]] = moved(second[steps[0] - 1], name, onward)
        elif kind == "tile":
            received = moved(other, name, over)
        elif kind == "swap":
            if steps == [0]:
                second[0] = moved(mine, name, across)
                continue
            parts = [x[i] for i in steps for x in ((first, second) if i < half else (first,))]
            both = moved(jnp.concatenate(parts), name, across)
            for n, i in enumerate(steps):
                swapped[i] = (both, 2 * n * shard)
        else:
            pieces, plan = [], []

            def add(x):
                if not any(x is y for y in pieces):
                    pieces.append(x)
                return next(n for n, y in enumerate(pieces) if x is y)

            for i in steps:
                if i == half:
                    plan.append((places(i), (add(first[i]), 0), (add(swapped[i][0]), swapped[i][1])))
                elif i >= 0:
                    plan.append((places(i), (add(first[i]), 0), (add(second[i]), 0)))
                else:
                    both, at = swapped[-i]
                    plan.append((places(i), (add(both), at + shard), (add(both), at)))
            terms = [own, received] if tile is None else [tile]
            last = half in steps
            direct = len(plan) if last else DIRECT if tile is None else 0
            out, blocks, tile = columns(
                plan, terms, pieces, shard, direct, ready if last else [], held if last else [], out, last,
                n_row * shard, COST.get(name, 1),
            )
            ready.append(blocks)
            held.append([(j, plan[j][0]) for j in range(direct, len(plan))])
            got[name] = blocks
    return out


def gather_body(g_occupied, g_virtual, owner, coulomb):
    n_col = lax.axis_size("col")
    pol = g_occupied.astype(jnp.float32) * g_virtual.astype(jnp.float32)
    columns = jnp.arange(n_col, dtype=jnp.int32)
    onehot = (owner[:, 0][:, None] == columns[None, :]).astype(jnp.float32)
    contrib = jnp.einsum("sd,sij->dij", onehot, pol).astype(jnp.bfloat16)
    received = lax.all_to_all(contrib, "col", split_axis=0, concat_axis=0, tiled=True)
    tile = jnp.sum(received.astype(jnp.float32), axis=0).astype(jnp.bfloat16)
    panel = lax.all_gather(coulomb, "row", axis=1, tiled=True)
    return jnp.dot(tile, panel, preferred_element_type=jnp.float32).astype(jnp.bfloat16)


def solution(mesh):
    ring = chip_ring(mesh) if mesh.shape["col"] == 2 else None
    if ring and ring[0] != CHIPS:
        ring = None
    return jax.shard_map(
        functools.partial(ring_body, ring) if ring else gather_body,
        mesh=mesh,
        in_specs=(P(AXES, None, None), P(AXES, None, None), P(AXES, None), P("col", "row")),
        out_specs=P(AXES, None),
        check_vma=False,
    )
```

```python
import functools
import math

import jax
import jax.numpy as jnp
import numpy as np
from jax import lax
from jax.experimental import pallas as pl
from jax.experimental.pallas import tpu as pltpu
from jax.sharding import PartitionSpec as P

AXES = ("row", "col")
ANY = pl.BlockSpec(memory_space=pl.ANY)
HBM = pl.BlockSpec(memory_space=pltpu.HBM)
VMEM = pl.BlockSpec(memory_space=pltpu.VMEM)

CHIPS = 8
ORDER = (
    "first_1",
    "first_2",
    "first_3",
    "first_4",
    "swap_0",
    "second_1",
    "second_2",
    "second_3",
    "tile",
    "swap_1_2",
    "swap_3",
    "chips_0_1_2_3",
    "swap_4",
    "chips_-1_-2_-3",
    "chips_4",
)
AFTER = {"swap_4": ("chips_0_1_2_3",), "first_2": ("own",)}
COST = {"chips_0_1_2_3": 8}
FRONT = 3221225472
DIRECT = 2


def chip_ring(mesh):
    n_row, n_col = mesh.devices.shape
    row_of = {}
    for r in range(n_row):
        for c in range(n_col):
            d = mesh.devices[r, c]
            row_of[(*d.coords, d.core_on_chip)] = (r, c)
    chips = sorted({k[:3] for k, (_, c) in row_of.items() if c == 0})
    if len(chips) * 2 != n_row:
        return None
    spans = [sorted({k[a] for k in chips}) for a in range(3)]
    wide = [a for a in range(3) if len(spans[a]) > 1]
    if len(wide) != 2 or math.prod(len(s) for s in spans) != len(chips):
        return None
    short, long = sorted(wide, key=lambda a: len(spans[a]))
    if len(spans[short]) != 2:
        return None
    lo, hi = spans[short]
    order = [(lo, v) for v in spans[long]] + [(hi, v) for v in reversed(spans[long])]
    place = {sv: i for i, sv in enumerate(order)}
    n = len(order)
    position = np.zeros((n_row, n_col), np.int32)
    core = np.zeros((n_row, n_col), np.int32)
    flat = {}
    for k, (r, c) in row_of.items():
        position[r, c] = place[(k[short], k[long])]
        core[r, c] = k[3]
        flat[(position[r, c], core[r, c], c)] = r * n_col + c
    slot = np.zeros((n_col, n), np.int32)
    for (p, k, c), f in flat.items():
        r = f // n_col
        if r % 2 != k:
            return None
        slot[c, p] = r // 2
    if (slot != slot[:1]).any():
        return None
    return n, position, core, flat, slot[0]


def tile_columns_kernel(n_col, out_ref):
    row = lax.broadcasted_iota(jnp.int32, out_ref.shape, 0)
    out_ref[...] = lax.rem(lax.axis_index("col") + row, n_col)


def tile_columns(n_col):
    return pl.pallas_call(
        functools.partial(tile_columns_kernel, n_col),
        out_shape=jax.ShapeDtypeStruct((8 * pl.cdiv(n_col, 8), 128), jnp.int32),
        out_specs=VMEM,
        cost_estimate=pl.CostEstimate(flops=FRONT, bytes_accessed=1 << 10, transcendentals=0),
        name="tile_columns",
    )()


def contribution_kernel(owner_ref, column_ref, occ_ref, vir_ref, *outs):
    pol = [occ_ref[p].astype(jnp.float32) * vir_ref[p].astype(jnp.float32) for p in range(occ_ref.shape[0])]
    lanes = column_ref.shape[1]
    for k, out in enumerate(outs):
        column = column_ref[pl.ds(k, 1)]
        picked = [jnp.where(owner_ref[:, p : p + 1] == column, 1.0, 0.0).astype(jnp.float32) for p in range(len(pol))]
        for at in range(0, out.shape[1], lanes):
            span = slice(at, at + lanes)
            total = pol[0][:, span] * picked[0]
            for p in range(1, len(pol)):
                total = total + pol[p][:, span] * picked[p]
            out[:, span] = total.astype(out.dtype)


def contributions(g_occupied, g_virtual, owner, column, n_col):
    pairs, rows, depth = g_occupied.shape
    return pl.pallas_call(
        contribution_kernel,
        out_shape=[jax.ShapeDtypeStruct((rows, depth), jnp.bfloat16)] * n_col,
        in_specs=[VMEM, VMEM, VMEM, VMEM],
        out_specs=[VMEM] * n_col,
        compiler_params=pltpu.CompilerParams(vmem_limit_bytes=24 << 20),
        cost_estimate=pl.CostEstimate(
            flops=4 * pairs * rows * depth, bytes_accessed=4 * pairs * rows * depth, transcendentals=0
        ),
        name="contributions",
    )(owner.reshape(1, pairs), column, g_occupied, g_virtual)


def columns_kernel(shard, n_terms, n_pieces, plan, direct, held, last, *refs):
    device = lax.axis_index("row")
    core = lax.rem(device, 2)
    width = 2 * shard
    refs = list(refs)
    terms = [refs.pop(0) for _ in range(n_terms)]
    pieces = [refs.pop(0) for _ in range(n_pieces)]
    ready = [refs.pop(0) for _ in held]
    sem, panel = refs.pop(), refs.pop()
    block = refs.pop()
    tile = terms[0] if n_terms == 1 else refs.pop()
    out = refs.pop() if refs else None
    copies = []

    def put(source, place, span):
        slot = place[0]
        for r, s in enumerate(place):
            slot = jnp.where(device == r, s, slot)
        at = pl.ds(pl.multiple_of(slot * width, width), width)
        copies.append(pltpu.make_async_copy(source.at[span], out.at[span, at], sem.at[len(copies)]))
        copies[-1].start()

    for blocks, places in zip(ready, held, strict=True):
        for j, place in places:
            put(blocks.at[j], place, pl.ds(0, tile.shape[0]))
    if n_terms == 2:
        tile[...] = (terms[0][...].astype(jnp.float32) + terms[1][...].astype(jnp.float32)).astype(tile.dtype)
    parts = 4 if last else 1
    rows = tile.shape[0] // parts
    step = 1 if n_terms == 2 else 2
    for j in range(0, len(plan), step):
        chips = list(range(j, min(j + step, len(plan))))
        for n in chips:
            _, here, there = plan[n]
            panel[n, core] = pieces[here[0]][pl.ds(here[1], shard)]
            panel[n, 1 - core] = pieces[there[0]][pl.ds(there[1], shard)]
        panels = panel[pl.ds(j, len(chips))].reshape(len(chips) * width, panel.shape[3])
        for i in range(parts):
            span = pl.ds(i * rows, rows)
            product = lax.dot_general(
                tile[span], panels, (((1,), (1,)), ((), ())), preferred_element_type=jnp.float32
            ).astype(block.dtype)
            for n in chips:
                block[n, span] = product[:, (n - j) * width : (n - j + 1) * width]
                if n < direct:
                    put(block.at[n], plan[n][0], span)
    for c in copies:
        c.wait()


def columns(plan, terms, pieces, shard, direct, ready, held, out, last, out_width, cost):
    rows, depth = terms[0].shape
    width = 2 * shard
    blocks = (len(plan), rows, width)
    args = [*terms, *pieces, *ready]
    in_specs = [VMEM] * len(args)
    aliases = {}
    if last and out is not None:
        aliases = {len(args): 0}
        args.append(out)
        in_specs.append(ANY)
    out_shape, out_specs = [], []
    if direct:
        out_shape.append(jax.ShapeDtypeStruct((rows, out_width), jnp.bfloat16))
        out_specs.append(ANY)
    if len(terms) == 2:
        out_shape.append(jax.ShapeDtypeStruct((rows, depth), jnp.bfloat16))
        out_specs.append(VMEM)
    if not last:
        out_shape.append(jax.ShapeDtypeStruct(blocks, jnp.bfloat16))
        out_specs.append(VMEM)
    n_in = len(args)

    def body(*refs):
        refs = list(refs)
        if aliases:
            del refs[n_in - 1]
        columns_kernel(shard, len(terms), len(pieces), plan, direct, held, last, *refs)

    result = pl.pallas_call(
        body,
        out_shape=out_shape,
        in_specs=in_specs,
        out_specs=out_specs,
        scratch_shapes=([pltpu.VMEM(blocks, jnp.bfloat16)] if last else [])
        + [
            pltpu.VMEM((len(plan), 2, shard, depth), jnp.bfloat16),
            pltpu.SemaphoreType.DMA((sum(len(h) for h in held) + 4 * len(plan),)),
        ],
        input_output_aliases=aliases,
        compiler_params=pltpu.CompilerParams(vmem_limit_bytes=16 << 20),
        cost_estimate=pl.CostEstimate(
            flops=cost * 2 * rows * depth * len(plan) * width,
            bytes_accessed=cost * len(plan) * width * rows * 2,
            transcendentals=0,
        ),
        name="columns",
    )(*args)
    result = list(result)
    out = result.pop(0) if direct else out
    tile = result.pop(0) if len(terms) == 2 else terms[0]
    return out, None if last else result.pop(0), tile


def after(x, *done):
    return lax.optimization_barrier((x, *done))[0]


def ring_body(ring, g_occupied, g_virtual, owner, coulomb):
    n_chips, position, core, flat, slot = ring
    n_row, n_col = position.shape
    half = n_chips // 2

    def pairs(step):
        out = []
        for r in range(n_row):
            for c in range(n_col):
                p, k = step(int(position[r, c]), int(core[r, c]))
                out.append((r * n_col + c, flat[(p % n_chips, k, c)]))
        return out

    onward = pairs(lambda p, k: (p + 1 - 2 * k, k))
    across = pairs(lambda p, k: (p, 1 - k))
    over = [(r * n_col + c, r * n_col + 1 - c) for r in range(n_row) for c in range(n_col)]

    def places(step):
        out = []
        for r in range(n_row):
            p, way = int(position[r, 0]), 1 - 2 * int(core[r, 0])
            out.append(int(slot[(p - way * step) % n_chips]))
        return out

    column = tile_columns(n_col)
    own, other = contributions(g_occupied, g_virtual, owner, column, n_col)
    mine = coulomb.T
    shard = mine.shape[0]
    first, second, swapped = {0: mine}, {}, {}
    got = {"own": own, "column": column}
    out, tile, ready, held = None, None, [], []

    def moved(x, name, way):
        with jax.named_scope(name):
            got[name] = lax.ppermute(after(x, *(got[n] for n in AFTER.get(name, ()))), AXES, way)
        return got[name]

    for name in ORDER:
        kind, *rest = name.split("_")
        steps = [int(i) for i in rest]
        if kind == "first":
            first[steps[0]] = moved(first[steps[0] - 1], name, onward)
        elif kind == "second":
            second[steps[0]] = moved(second[steps[0] - 1], name, onward)
        elif kind == "tile":
            received = moved(other, name, over)
        elif kind == "swap":
            if steps == [0]:
                second[0] = moved(mine, name, across)
                continue
            parts = [x[i] for i in steps for x in ((first, second) if i < half else (first,))]
            both = moved(jnp.concatenate(parts), name, across)
            for n, i in enumerate(steps):
                swapped[i] = (both, 2 * n * shard)
        else:
            pieces, plan = [], []

            def add(x):
                if not any(x is y for y in pieces):
                    pieces.append(x)
                return next(n for n, y in enumerate(pieces) if x is y)

            for i in steps:
                if i == half:
                    plan.append((places(i), (add(first[i]), 0), (add(swapped[i][0]), swapped[i][1])))
                elif i >= 0:
                    plan.append((places(i), (add(first[i]), 0), (add(second[i]), 0)))
                else:
                    both, at = swapped[-i]
                    plan.append((places(i), (add(both), at + shard), (add(both), at)))
            terms = [own, received] if tile is None else [tile]
            last = half in steps
            direct = len(plan) if last else DIRECT if tile is None else 0
            out, blocks, tile = columns(
                plan, terms, pieces, shard, direct, ready if last else [], held if last else [], out, last,
                n_row * shard, COST.get(name, 1),
            )
            ready.append(blocks)
            held.append([(j, plan[j][0]) for j in range(direct, len(plan))])
            got[name] = blocks
    return out


def gather_body(g_occupied, g_virtual, owner, coulomb):
    n_col = lax.axis_size("col")
    pol = g_occupied.astype(jnp.float32) * g_virtual.astype(jnp.float32)
    columns = jnp.arange(n_col, dtype=jnp.int32)
    onehot = (owner[:, 0][:, None] == columns[None, :]).astype(jnp.float32)
    contrib = jnp.einsum("sd,sij->dij", onehot, pol).astype(jnp.bfloat16)
    received = lax.all_to_all(contrib, "col", split_axis=0, concat_axis=0, tiled=True)
    tile = jnp.sum(received.astype(jnp.float32), axis=0).astype(jnp.bfloat16)
    panel = lax.all_gather(coulomb, "row", axis=1, tiled=True)
    return jnp.dot(tile, panel, preferred_element_type=jnp.float32).astype(jnp.bfloat16)


def solution(mesh):
    ring = chip_ring(mesh) if mesh.shape["col"] == 2 else None
    if ring and ring[0] != CHIPS:
        ring = None
    return jax.shard_map(
        functools.partial(ring_body, ring) if ring else gather_body,
        mesh=mesh,
        in_specs=(P(AXES, None, None), P(AXES, None, None), P(AXES, None), P("col", "row")),
        out_specs=P(AXES, None),
        check_vma=False,
    )
```
